256 devices in a mesh: gz: 8 (over z_hi, y), spec: 32 (over z_lo, x, core).
Axes of the slice: x: 4, y: 4, z: 8 (z_hi: 2, z_lo: 4; z = z_hi * 4 + z_lo), core: 2. Of those that a mesh axis runs over, the one named last changes fastest.
Arguments:
- flux: bfloat16 [8192, 7168], P('spec', 'gz'), may hold values from -6 to 6
- ivar: bfloat16 [8192, 7168], P('spec', 'gz'), may hold values from 0.25 to 4
- mask: int32 [8192, 7168], P('spec', 'gz'), may hold values 0 or 1
- table: bfloat16 [7168, 4, 1024], P('spec', None, 'gz'), may hold values from -6 to 6
Outputs:
- decrease: float32 [8192, 1024], P('spec', 'gz')
- best: float32 [8192], P('spec')
The draws below stay inside these ranges and needn't reach their ends.
Inputs may be any that keep to these rules, and one draw needn't show every extreme that they name: `mask`: 1 marks a good pixel, 0 a masked one.
All inputs are finite; a program needn't handle non-finite values. No bound on the sum of `mask` on one device may be relied on, other than what follows from the above.
Results may differ from the reference program's by a relative error of at most 0.0024.
Values may be sent and summed in bfloat16 or wider, within the bound.
No kernel may reach another device: no remote copies, remote signals or barrier semaphores. Data moves between devices by JAX's collectives and lax.ppermute only.
A program may use at most 128 MiB of HBM per device.

```python
import math
import jax
import jax.numpy as jnp
from jax import lax

WAVE = 7168
COMP = 4
SDEV = 256
SPECTRA = 8192
ZGRID = 1024


def with_ends(result, rng, low, high):
    longest = result.shape.index(max(result.shape))
    spots = []
    for shift in (0, 1):
        where = [jax.random.randint(jax.random.fold_in(rng, axis), (), 0, length) for axis, length in enumerate(result.shape)]
        where[longest] = (where[longest] + shift) % result.shape[longest]
        spots.append(tuple(where))
    return result.at[spots[0]].set(low).at[spots[1]].set(high)


def block_levels(key, dims, split, smallest, top_value):
    gain = 1.0
    for dim, shards_of in split:
        steps = jax.random.uniform(jax.random.fold_in(jax.random.fold_in(key, 6), dim), (shards_of,), jnp.float32, smallest / len(split), top_value / len(split))
        gain = gain * jnp.repeat(jnp.exp(steps), dims[dim] // shards_of).reshape((-1,) + (1,) * (len(dims) - 1 - dim))
    return gain


def noise(rng, dims, scale, bound, shards=(), kind=jnp.bfloat16):
    array = jax.random.normal(rng, dims, jnp.float32) * scale
    if len(shards) > 0:
        array = block_levels(rng, dims, shards, -0.22, 0.18) * array
    return jnp.clip(array, min=-bound, max=bound).astype(kind)


def setup_inputs(seed: int = 0) -> dict:
    keys = jax.random.split(jax.random.key(seed), 5)
    return {
        "flux": noise(keys[0], (SPECTRA, WAVE), 1.0, 6.0, ((0, 32), (1, 8))),
        "ivar": jnp.clip(jnp.exp(math.log(4.0) - 2.7725887 * jax.random.uniform(keys[1], (SPECTRA, WAVE), jnp.float32) ** block_levels(keys[1], (SPECTRA, WAVE), ((0, 32), (1, 8)), -0.2, 0.2)), 0.25, 4.0).astype(jnp.bfloat16),
        "mask": with_ends((jax.random.randint(keys[2], (SPECTRA, WAVE), 0, 8) < 7).astype(jnp.int32), jax.random.fold_in(keys[2], 1), 0, 1),
        "table": noise(keys[3], (WAVE, COMP, ZGRID), 1.0, 6.0, ((0, 32), (2, 8))),
    }


PAIR_LIST = ((0, 0), (0, 1), (0, 2), (0, 3), (1, 1), (1, 2), (1, 3), (2, 2), (2, 3), (3, 3))

def pair_table(templates):
    columns = [templates[:, i, :].astype(jnp.float32) * templates[:, j, :].astype(jnp.float32) for i, j in PAIR_LIST]
    return jnp.stack(columns, axis=1).astype(jnp.bfloat16)

def fit_gain(gram, proj):
    where = {}
    for number, pair in enumerate(PAIR_LIST):
        where[pair] = number
    lower = {}
    for j in range(4):
        diag = gram[:, where[j, j], :]
        for k in range(j):
            diag = diag - lower[j, k] * lower[j, k]
        lower[j, j] = jnp.sqrt(diag)
        for i in range(j + 1, 4):
            entry = gram[:, where[j, i], :]
            for k in range(j):
                entry = entry - lower[i, k] * lower[j, k]
            lower[i, j] = entry / lower[j, j]
    solved = []
    total = jnp.zeros(proj[:, 0, :].shape, jnp.float32)
    for i in range(4):
        value = proj[:, i, :]
        for k in range(i):
            value = value - lower[i, k] * solved[k]
        value = value / lower[i, i]
        solved.append(value)
        total = total + value * value
    return total

def reference(flux, ivar, mask, table):
    ivar_f = ivar.astype(jnp.float32)
    mask_f = mask.astype(jnp.float32)
    weight = (ivar_f * mask_f).astype(jnp.bfloat16)
    weighted = (flux.astype(jnp.float32) * ivar_f * mask_f).astype(jnp.bfloat16)
    wave_count = table.shape[0]
    grid = table.shape[2]
    flat_table = table.reshape(wave_count, 4 * grid)
    flat_pairs = pair_table(table).reshape(wave_count, 10 * grid)
    count = flux.shape[0]

    def one_block(block):
        part_weighted, part_weight = block
        proj = jnp.dot(part_weighted, flat_table, preferred_element_type=jnp.float32).reshape(-1, 4, grid)
        gram = jnp.dot(part_weight, flat_pairs, preferred_element_type=jnp.float32).reshape(-1, 10, grid)
        return fit_gain(gram, proj)
    blocks = (weighted.reshape(count // SDEV, SDEV, wave_count), weight.reshape(count // SDEV, SDEV, wave_count))
    decrease = lax.map(one_block, blocks).reshape(count, grid)
    best = lax.optimization_barrier(jnp.max(decrease, axis=1))
    return (decrease, best)
```

```python
import jax
import jax.numpy as jnp
from jax import lax
from jax.experimental import pallas as pl
from jax.experimental.pallas import tpu as pltpu
from jax.sharding import PartitionSpec as P

PAIR_LIST = ((0, 0), (0, 1), (0, 2), (0, 3), (1, 1), (1, 2), (1, 3), (2, 2), (2, 3), (3, 3))
AXES = ("gz", "spec")
NZH, NY, NZL, NX = 2, 4, 4, 4


def place(i):
    gz, spec = divmod(i, NZL * NX * 2)
    zh, y = divmod(gz, NY)
    zl, r = divmod(spec, NX * 2)
    x, c = divmod(r, 2)
    return zh, y, zl, x, c


def number(zh, y, zl, x, c):
    return ((zh % NZH) * NY + y % NY) * NZL * NX * 2 + (zl % NZL) * NX * 2 + (x % NX) * 2 + c % 2


def shift(value, dh=0, dy=0, dl=0, dx=0, dc=0):
    pairs = []
    for i in range(NZH * NY * NZL * NX * 2):
        zh, y, zl, x, c = place(i)
        pairs.append((i, number(zh + dh, y + dy, zl + dl, x + dx, c + dc)))
    return lax.ppermute(value, AXES, pairs)


def fit_gain(gram, proj):
    where = {}
    for n, pair in enumerate(PAIR_LIST):
        where[pair] = n
    lower = {}
    for j in range(4):
        diag = gram(where[j, j])
        for k in range(j):
            diag = diag - lower[j, k] * lower[j, k]
        lower[j, j] = jnp.sqrt(diag)
        for i in range(j + 1, 4):
            entry = gram(where[j, i])
            for k in range(j):
                entry = entry - lower[i, k] * lower[j, k]
            lower[i, j] = entry / lower[j, j]
    solved = []
    total = None
    for i in range(4):
        value = proj(i)
        for k in range(i):
            value = value - lower[i, k] * solved[k]
        value = value / lower[i, i]
        solved.append(value)
        total = value * value if total is None else total + value * value
    return total


def scan_kernel(where_ref, *refs):
    rows = refs[:16]
    tables = refs[16:24]
    dec_ref, top_ref = refs[24:26]
    wd, wt, tab, acc, row_sem, tab_sem = refs[26:]
    zh, y, zl, x, c = (where_ref[i] for i in range(5))
    shard = tab.shape[0] // 32
    chunk = 4 * shard

    def table_copy(src, s):
        at = pl.multiple_of(s * shard, shard)
        return pltpu.make_async_copy(src, tab.at[pl.ds(at, shard), :], tab_sem.at[s])

    def row_copy(n, array):
        return pltpu.make_async_copy(rows[2 * n + array], (wd, wt)[array].at[n], row_sem.at[n, array])

    for n in range(8):
        for array in range(2):
            row_copy(n, array).start()
    for k in range(4):
        for j, dx in enumerate((0, -1, 1, 2)):
            for other in range(2):
                s = ((zl - k) % 4) * 8 + ((x + dx) % 4) * 2 + (c + other) % 2
                table_copy(tables[2 * k + other].at[pl.ds(j * shard, shard), :], s).start()
    acc[...] = jnp.zeros_like(acc)

    def step(n, carry):
        for array in range(2):
            pltpu.make_async_copy(rows[array], (wd, wt)[array].at[n], row_sem.at[n, array]).wait()
        h, d = n // 4, n % 4
        dy = jnp.where(d == 0, 0, jnp.where(d == 1, -1, jnp.where(d == 2, 1, 2)))
        g = ((zh + h) % 2) * 4 + (y + dy) % 4
        for q in range(4):
            table_copy(tables[0].at[pl.ds(0, shard), :], 4 * g + q).wait()
        at = pl.multiple_of(g * chunk, chunk)

        def comp(i):
            return tab[pl.ds(at, chunk), i * 128:(i + 1) * 128]

        left = wd[n]
        for t in range(2):
            acc[:, t * 256:(t + 1) * 256] += jnp.dot(
                left, tab[pl.ds(at, chunk), t * 256:(t + 1) * 256], preferred_element_type=jnp.float32)
        left = wt[n]
        for t in range(5):
            (a, b), (e, f) = PAIR_LIST[2 * t], PAIR_LIST[2 * t + 1]
            right = jnp.concatenate([comp(a) * comp(b), comp(e) * comp(f)], axis=1)
            acc[:, 512 + t * 256:512 + (t + 1) * 256] += jnp.dot(
                left, right, preferred_element_type=jnp.float32)
        return carry

    lax.fori_loop(0, 8, step, 0)
    total = fit_gain(lambda p: acc[:, 512 + p * 128:512 + (p + 1) * 128],
                     lambda k: acc[:, k * 128:(k + 1) * 128])
    dec_ref[...] = total
    top = jnp.max(total.T, axis=0, keepdims=True)
    top_ref[...] = jnp.broadcast_to(top, top_ref.shape)


def scan(where, rows, tables):
    spectra, chunk = rows[0].shape
    shard = chunk // 4
    return pl.pallas_call(
        scan_kernel,
        out_shape=(jax.ShapeDtypeStruct((spectra, 128), jnp.float32),
                   jax.ShapeDtypeStruct((8, spectra), jnp.float32)),
        in_specs=[pl.BlockSpec(memory_space=pltpu.SMEM)]
        + [pl.BlockSpec(memory_space=pl.ANY)] * 24,
        out_specs=(pl.BlockSpec(memory_space=pltpu.VMEM), pl.BlockSpec(memory_space=pltpu.VMEM)),
        scratch_shapes=[
            pltpu.VMEM((8, spectra, chunk), jnp.bfloat16),
            pltpu.VMEM((8, spectra, chunk), jnp.bfloat16),
            pltpu.VMEM((32 * shard, 512), jnp.bfloat16),
            pltpu.VMEM((spectra, 14 * 128), jnp.float32),
            pltpu.SemaphoreType.DMA((8, 2)),
            pltpu.SemaphoreType.DMA((32,)),
        ],
        compiler_params=pltpu.CompilerParams(vmem_limit_bytes=48 << 20),
        cost_estimate=pl.CostEstimate(flops=2 * spectra * 8 * chunk * 1792, bytes_accessed=16 << 20, transcendentals=0),
    )(where, *rows, *tables)


def spread_y(wd, wt):
    up_wd, up_wt = shift(wd, dy=1), shift(wt, dy=1)
    down_wd, down_wt = shift(wd, dy=-1), shift(wt, dy=-1)
    far_wd, far_wt = shift(up_wd, dy=1), shift(down_wt, dy=-1)
    return [wd, wt, up_wd, up_wt, down_wd, down_wt, far_wd, far_wt]


def local(flux, ivar, mask, table):
    ivar_f = ivar.astype(jnp.float32)
    mask_f = mask.astype(jnp.float32)
    wt = (ivar_f * mask_f).astype(jnp.bfloat16)
    wd = (flux.astype(jnp.float32) * ivar_f * mask_f).astype(jnp.bfloat16)
    shard = table.shape[0]
    flat = table.reshape(shard, 4 * table.shape[2])
    rows = spread_y(wd, wt)
    rows += spread_y(shift(wd, dh=1), shift(wt, dh=1))
    tables = []
    for k in range(4):
        block = flat if k == 0 else shift(flat, dl=k)
        both = jnp.concatenate([block, shift(block, dx=1), shift(block, dx=-1), shift(block, dx=2)], axis=0)
        tables += [both, shift(both, dc=1)]
    gz, spec = lax.axis_index("gz"), lax.axis_index("spec")
    where = jnp.stack([gz // 4, gz % 4, spec // 8, spec // 2 % 4, spec % 2]).astype(jnp.int32)
    decrease, top = scan(where, rows, tables)
    tops = lax.all_to_all(top, "gz", 0, 0, tiled=True)
    return decrease, jnp.max(tops, axis=0)


def solution(mesh):
    placed = (P("spec", "gz"), P("spec", "gz"), P("spec", "gz"), P("spec", None, "gz"))
    return jax.shard_map(
        local, mesh=mesh, in_specs=placed, out_specs=(P("spec", "gz"), P("spec")), check_vma=False
    )
```

```python
import functools

import jax
import jax.numpy as jnp
from jax import lax
from jax.experimental import pallas as pl
from jax.experimental.pallas import tpu as pltpu
from jax.sharding import PartitionSpec as P


PAIR_LIST = ((0, 0), (0, 1), (0, 2), (0, 3), (1, 1), (1, 2), (1, 3), (2, 2), (2, 3), (3, 3))
AXES = ("gz", "spec")
NZH, NY, NZL, NX = 2, 4, 4, 4
STEPS_Y = (0, -1, 1, 2)
STEPS_X = (0, -1, 1, 2)
CUT = 640


def place(i):
    gz, spec = divmod(i, NZL * NX * 2)
    zh, y = divmod(gz, NY)
    zl, r = divmod(spec, NX * 2)
    x, c = divmod(r, 2)
    return zh, y, zl, x, c


def number(zh, y, zl, x, c):
    return ((zh % NZH) * NY + y % NY) * NZL * NX * 2 + (zl % NZL) * NX * 2 + (x % NX) * 2 + c % 2


def shift(value, dh=0, dy=0, dl=0, dx=0, dc=0):
    pairs = []
    for i in range(NZH * NY * NZL * NX * 2):
        zh, y, zl, x, c = place(i)
        pairs.append((i, number(zh + dh, y + dy, zl + dl, x + dx, c + dc)))
    return lax.ppermute(value, AXES, pairs)


def fit_gain(gram, proj):
    where = {}
    for n, pair in enumerate(PAIR_LIST):
        where[pair] = n
    lower = {}
    for j in range(4):
        diag = gram(where[j, j])
        for k in range(j):
            diag = diag - lower[j, k] * lower[j, k]
        lower[j, j] = jnp.sqrt(diag)
        for i in range(j + 1, 4):
            entry = gram(where[j, i])
            for k in range(j):
                entry = entry - lower[i, k] * lower[j, k]
            lower[i, j] = entry / lower[j, j]
    solved = []
    total = None
    for i in range(4):
        value = proj(i)
        for k in range(i):
            value = value - lower[i, k] * solved[k]
        value = value / lower[i, i]
        solved.append(value)
        total = value * value if total is None else total + value * value
    return total


def pair_products(m, left, tab, acc):
    lhs = left[m, 0]
    for t in range(2):
        at = slice(t * 256, (t + 1) * 256)
        acc[:, at] += jnp.dot(lhs, tab[m, :, at], preferred_element_type=jnp.float32)
    lhs = left[m, 1]

    def comp(i):
        return tab[m, :, i * 128:(i + 1) * 128]

    for t in range(5):
        (a, b), (e, f) = PAIR_LIST[2 * t], PAIR_LIST[2 * t + 1]
        right = jnp.concatenate([comp(a) * comp(b), comp(e) * comp(f)], axis=1)
        at = slice(512 + t * 256, 512 + (t + 1) * 256)
        acc[:, at] += jnp.dot(lhs, right, preferred_element_type=jnp.float32)


def multiply(half, span, places, where_ref, rows, tables, acc, left, tab, row_sem, tab_sem):
    zh, y, zl, x, c = (where_ref[i] for i in range(5))
    shard = tables[0].shape[0]
    first, width = span
    near, mid, far = tables[:8], tables[8:16], tables[16:]
    pieces = []
    for q in range(4):
        low, high = max(first, q * shard), min(first + width, (q + 1) * shard)
        pieces.append((low - q * shard, high - low, low - first) if low < high else None)

    def table_copy(src, base, n, q):
        start, size, to = pieces[q]
        at = pl.multiple_of((n % 2) * width + to, 32)
        return pltpu.make_async_copy(
            src.at[pl.ds(base + start, size), :], tab.at[n // 2, pl.ds(at, size), :], tab_sem.at[n, q])

    plan = [[] for _ in range(4)]
    for m, (n, array) in enumerate(places):
        lanes = pl.ds((n % 2) * width, width)
        arrays = pl.ds(0, 2) if array is None else array
        plan[n].append(pltpu.make_async_copy(rows[m], left.at[n // 2, arrays, :, lanes], row_sem.at[m]))

    def start_rows(n):
        for copy in plan[n]:
            copy.start()

    start_rows(0)
    start_rows(1)
    for k in range(4):
        zs = (zl + 4 - k) % 4

        @pl.when(zs // 2 == (zh + half) % 2)
        def _(k=k, zs=zs):
            for j, dx in enumerate(STEPS_X):
                xs = (x + 4 + dx) % 4
                dy = ((zs % 2) * 2 + xs // 2 + 4 - y) % 4
                n = jnp.where(dy == 0, 0, jnp.where(dy == 3, 1, jnp.where(dy == 1, 2, 3)))
                for other in range(2):
                    src = (near, mid, mid, far)[k][2 * j + other]
                    base = shard if k == 2 else 0
                    mine = (xs % 2) * 2 + (c + other) % 2
                    if width == 4 * shard:
                        at = pl.multiple_of((n % 2) * width + mine * shard, 32)
                        pltpu.make_async_copy(
                            src.at[pl.ds(base, shard), :], tab.at[n // 2, pl.ds(at, shard), :], tab_sem.at[n, mine]).start()
                        continue
                    for q in range(4):
                        if pieces[q] is not None:
                            @pl.when(mine == q)
                            def _(src=src, base=base, n=n, q=q):
                                table_copy(src, base, n, q).start()
    start_rows(2)
    start_rows(3)
    for m in range(2):
        for n in (2 * m, 2 * m + 1):
            for copy in plan[n]:
                copy.wait()
            for q in range(4):
                if pieces[q] is not None:
                    table_copy(far[0], 0, n, q).wait()
        pair_products(m, left, tab, acc)


def block_kernel(second, n_rows, n_tables, n_sums, where_ref, *refs):
    rows, tables = refs[:n_rows], refs[n_rows:n_rows + n_tables]
    before = refs[n_rows + n_tables:n_rows + n_tables + n_sums]
    acc, left, tab, row_sem, tab_sem = refs[n_rows + n_tables + n_sums:]
    zh, y, zl, x, c = (where_ref[i] for i in range(5))
    shard = tables[0].shape[0] if not second else tables[8].shape[0]
    width = 4 * shard
    wanted = jnp.where(zl // 2 == zh, zl, (zl + 2) % 4)
    if second:
        wanted = wanted + 1 - 2 * (wanted % 2)

    def row_copy(src, slot, array):
        lanes = pl.ds(pl.multiple_of(slot * width, 128), width)
        return pltpu.make_async_copy(src, left.at[0, array, :, lanes], row_sem.at[slot, array])

    def table_copy(src, base, slot, q):
        at = pl.multiple_of(slot * width + q * shard, 32)
        return pltpu.make_async_copy(src.at[pl.ds(base, shard), :], tab.at[0, pl.ds(at, shard), :], tab_sem.at[slot, q])

    for n, dy in enumerate(STEPS_Y):
        chunk = (y + 4 + dy) % 4

        @pl.when(chunk // 2 == wanted % 2)
        def _(n=n, chunk=chunk):
            for array in range(2):
                src = rows[3 + array] if n == 3 else rows[n].at[array]
                row_copy(src, chunk % 2, array).start()
    for k, group, base in (((1, 0, 0), (3, 1, 0)) if second else ((0, 0, 0), (2, 1, 1))):
        @pl.when((zl + 4 - k) % 4 == wanted)
        def _(group=group, base=base):
            for j, dx in enumerate(STEPS_X):
                xs = (x + 4 + dx) % 4
                for other in range(2):
                    src = tables[8 * group + 2 * j + other]
                    table_copy(src, base * shard, xs // 2, (xs % 2) * 2 + (c + other) % 2).start()
    acc[...] = before[0][...] if before else jnp.zeros_like(acc)
    for slot in range(2):
        for array in range(2):
            row_copy(rows[3], slot, array).wait()
        for q in range(4):
            table_copy(tables[0], 0, slot, q).wait()
    pair_products(0, left, tab, acc)


def sum_kernel(half, span, places, n_tables, n_sums, where_ref, *refs):
    rows, tables = refs[:len(places)], refs[len(places):len(places) + n_tables]
    before, (sum_ref, *scratch) = refs[len(places) + n_tables:][:n_sums], refs[len(places) + n_tables + n_sums:]
    sum_ref[...] = before[0][...]
    multiply(half, span, places, where_ref, rows, tables, sum_ref, *scratch)


def last_kernel(half, span, places, n_tables, where_ref, *refs):
    rows, tables = refs[:len(places)], refs[len(places):len(places) + n_tables]
    before_ref, dec_ref, top_ref, acc, *scratch = refs[len(places) + n_tables:]
    acc[...] = before_ref[...]
    multiply(half, span, places, where_ref, rows, tables, acc, *scratch)
    tall = 32

    def fit(b, carry):
        at = pl.ds(pl.multiple_of(b * tall, tall), tall)
        dec_ref[at, :] = fit_gain(lambda p: acc[at, 512 + p * 128:512 + (p + 1) * 128],
                                  lambda k: acc[at, k * 128:(k + 1) * 128])
        return carry

    lax.fori_loop(0, acc.shape[0] // tall, fit, 0)
    top = jnp.max(dec_ref[...].T, axis=0, keepdims=True)
    top_ref[...] = jnp.broadcast_to(top, top_ref.shape)


def run(kernel, where, rows, tables, sums, outs, pairs, height, width, keep=()):
    vmem = pl.BlockSpec(memory_space=pltpu.VMEM)
    return pl.pallas_call(
        kernel,
        out_shape=outs,
        in_specs=[pl.BlockSpec(memory_space=pltpu.SMEM)]
        + [pl.BlockSpec(memory_space=pl.ANY)] * (len(rows) + len(tables)) + [vmem] * len(sums),
        out_specs=(vmem,) * len(outs),
        scratch_shapes=list(keep) + [
            pltpu.VMEM((pairs, 2, height, 2 * width), jnp.bfloat16),
            pltpu.VMEM((pairs, 2 * width, 512), jnp.bfloat16),
            pltpu.SemaphoreType.DMA((2, 2) if pairs == 1 else (len(rows),)),
            pltpu.SemaphoreType.DMA((2 * pairs, 4)),
        ],
        compiler_params=pltpu.CompilerParams(vmem_limit_bytes=24 << 20),
        cost_estimate=pl.CostEstimate(
            flops=2 * height * 2 * pairs * width * 1792, bytes_accessed=pairs << 22, transcendentals=0),
    )(where, *rows, *tables, *sums)


def spread_x(block):
    return [block] + [shift(block, dx=dx) for dx in (1, -1, 2)]


def spread_and_fit(flux, ivar, mask, table):
    gz, spec = lax.axis_index("gz"), lax.axis_index("spec")
    where = jnp.stack([gz // 4, gz % 4, spec // 8, spec // 2 % 4, spec % 2]).astype(jnp.int32)
    shard = table.shape[0]
    flat = table.reshape(shard, 4 * table.shape[2])
    ivar_f = ivar.astype(jnp.float32)
    mask_f = mask.astype(jnp.float32)
    wt = (ivar_f * mask_f).astype(jnp.bfloat16)
    wd = (flux.astype(jnp.float32) * ivar_f * mask_f).astype(jnp.bfloat16)
    own = jnp.stack([wd, wt])

    two = jnp.concatenate([shift(flat, dl=1), shift(flat, dl=2)], axis=0)
    last = shift(flat, dl=3)
    tables = []
    for block in (flat, two, last):
        for piece in spread_x(block):
            tables += [piece, shift(piece, dc=1)]

    yu, yd = shift(own, dy=1), shift(own, dy=-1)
    fu, fd = shift(yu[0], dy=1), shift(yd[1], dy=-1)
    za, zb = shift(own[:, :, :CUT], dh=1), shift(own[:, :, CUT:], dh=1)
    ua, da, ya = shift(za, dy=1), shift(za, dy=-1), shift(za, dy=2)
    ub, db, yb = shift(zb, dy=1), shift(zb, dy=-1), shift(zb, dy=2)

    spectra, width = wt.shape
    sums = jax.ShapeDtypeStruct((spectra, 14 * 128), jnp.float32)
    near, mid, far = tables[:8], tables[8:16], tables[16:]
    rows = [own, yu, yd, fu, fd]
    total, = run(functools.partial(block_kernel, False, 5, 16, 0), where, rows, near + mid, [],
                 (sums,), 1, spectra, width)
    total, = run(functools.partial(block_kernel, True, 5, 16, 1), where, rows, mid + far, [total],
                 (sums,), 1, spectra, width)
    places = [(n, None) for n in range(4)]
    total, = run(functools.partial(sum_kernel, 1, (0, CUT), places, 24, 1), where, [za, ua, da, ya],
                 tables, [total], (sums,), 2, spectra, CUT)
    decrease, top = run(
        functools.partial(last_kernel, 1, (CUT, width - CUT), places, 24), where, [zb, ub, db, yb], tables, [total],
        (jax.ShapeDtypeStruct((spectra, 128), jnp.float32), jax.ShapeDtypeStruct((8, spectra), jnp.float32)),
        2, spectra, width - CUT, keep=[pltpu.VMEM(sums.shape, sums.dtype)])
    tops = lax.all_to_all(top, "gz", 0, 0, tiled=True)
    return decrease, jnp.max(tops, axis=0)


def solution(mesh):
    placed = (P("spec", "gz"), P("spec", "gz"), P("spec", "gz"), P("spec", None, "gz"))
    return jax.shard_map(
        spread_and_fit, mesh=mesh, in_specs=placed, out_specs=(P("spec", "gz"), P("spec")), check_vma=False
    )
```

```python
import functools

import jax
import jax.numpy as jnp
from jax import lax
from jax.experimental import pallas as pl
from jax.experimental.pallas import tpu as pltpu
from jax.sharding import PartitionSpec as P


PAIR_LIST = ((0, 0), (0, 1), (0, 2), (0, 3), (1, 1), (1, 2), (1, 3), (2, 2), (2, 3), (3, 3))
AXES = ("gz", "spec")
NZH, NY, NZL, NX = 2, 4, 4, 4
STEPS_Y = (0, -1, 1, 2)
STEPS_X = (0, -1, 1, 2)
CUT = 640


def place(i):
    gz, spec = divmod(i, NZL * NX * 2)
    zh, y = divmod(gz, NY)
    zl, r = divmod(spec, NX * 2)
    x, c = divmod(r, 2)
    return zh, y, zl, x, c


def number(zh, y, zl, x, c):
    return ((zh % NZH) * NY + y % NY) * NZL * NX * 2 + (zl % NZL) * NX * 2 + (x % NX) * 2 + c % 2


def shift(value, dh=0, dy=0, dl=0, dx=0, dc=0):
    pairs = []
    for i in range(NZH * NY * NZL * NX * 2):
        zh, y, zl, x, c = place(i)
        pairs.append((i, number(zh + dh, y + dy, zl + dl, x + dx, c + dc)))
    return lax.ppermute(value, AXES, pairs)


def fit_gain(gram, proj):
    where = {}
    for n, pair in enumerate(PAIR_LIST):
        where[pair] = n
    lower = {}
    for j in range(4):
        diag = gram(where[j, j])
        for k in range(j):
            diag = diag - lower[j, k] * lower[j, k]
        lower[j, j] = jnp.sqrt(diag)
        for i in range(j + 1, 4):
            entry = gram(where[j, i])
            for k in range(j):
                entry = entry - lower[i, k] * lower[j, k]
            lower[i, j] = entry / lower[j, j]
    solved = []
    total = None
    for i in range(4):
        value = proj(i)
        for k in range(i):
            value = value - lower[i, k] * solved[k]
        value = value / lower[i, i]
        solved.append(value)
        total = value * value if total is None else total + value * value
    return total


def pair_products(m, left, tab, acc):
    lhs = left[m, 0]
    for t in range(2):
        at = slice(t * 256, (t + 1) * 256)
        acc[:, at] += jnp.dot(lhs, tab[m, :, at], preferred_element_type=jnp.float32)
    lhs = left[m, 1]

    def comp(i):
        return tab[m, :, i * 128:(i + 1) * 128]

    for t in range(5):
        (a, b), (e, f) = PAIR_LIST[2 * t], PAIR_LIST[2 * t + 1]
        right = jnp.concatenate([comp(a) * comp(b), comp(e) * comp(f)], axis=1)
        at = slice(512 + t * 256, 512 + (t + 1) * 256)
        acc[:, at] += jnp.dot(lhs, right, preferred_element_type=jnp.float32)


def multiply(half, span, places, where_ref, rows, tables, acc, left, tab, row_sem, tab_sem):
    zh, y, zl, x, c = (where_ref[i] for i in range(5))
    shard = tables[0].shape[0]
    first, width = span
    near, mid, far = tables[:8], tables[8:16], tables[16:]
    pieces = []
    for q in range(4):
        low, high = max(first, q * shard), min(first + width, (q + 1) * shard)
        pieces.append((low - q * shard, high - low, low - first) if low < high else None)

    def table_copy(src, base, n, q):
        start, size, to = pieces[q]
        at = pl.multiple_of((n % 2) * width + to, 32)
        return pltpu.make_async_copy(
            src.at[pl.ds(base + start, size), :], tab.at[n // 2, pl.ds(at, size), :], tab_sem.at[n, q])

    plan = [[] for _ in range(4)]
    for m, (n, array) in enumerate(places):
        lanes = pl.ds((n % 2) * width, width)
        arrays = pl.ds(0, 2) if array is None else array
        plan[n].append(pltpu.make_async_copy(rows[m], left.at[n // 2, arrays, :, lanes], row_sem.at[m]))

    def start_rows(n):
        for copy in plan[n]:
            copy.start()

    start_rows(0)
    start_rows(1)
    for k in range(4):
        zs = (zl + 4 - k) % 4

        @pl.when(zs // 2 == (zh + half) % 2)
        def _(k=k, zs=zs):
            for j, dx in enumerate(STEPS_X):
                xs = (x + 4 + dx) % 4
                dy = ((zs % 2) * 2 + xs // 2 + 4 - y) % 4
                n = jnp.where(dy == 0, 0, jnp.where(dy == 3, 1, jnp.where(dy == 1, 2, 3)))
                for other in range(2):
                    src = (near, mid, mid, far)[k][2 * j + other]
                    base = shard if k == 2 else 0
                    mine = (xs % 2) * 2 + (c + other) % 2
                    if width == 4 * shard:
                        at = pl.multiple_of((n % 2) * width + mine * shard, 32)
                        pltpu.make_async_copy(
                            src.at[pl.ds(base, shard), :], tab.at[n // 2, pl.ds(at, shard), :], tab_sem.at[n, mine]).start()
                        continue
                    for q in range(4):
                        if pieces[q] is not None:
                            @pl.when(mine == q)
                            def _(src=src, base=base, n=n, q=q):
                                table_copy(src, base, n, q).start()
    start_rows(2)
    start_rows(3)
    for m in range(2):
        for n in (2 * m, 2 * m + 1):
            for copy in plan[n]:
                copy.wait()
            for q in range(4):
                if pieces[q] is not None:
                    table_copy(far[0], 0, n, q).wait()
        pair_products(m, left, tab, acc)


def block_kernel(second, n_rows, n_tables, n_sums, where_ref, *refs):
    rows, tables = refs[:n_rows], refs[n_rows:n_rows + n_tables]
    before = refs[n_rows + n_tables:n_rows + n_tables + n_sums]
    acc, left, tab, row_sem, tab_sem = refs[n_rows + n_tables + n_sums:]
    zh, y, zl, x, c = (where_ref[i] for i in range(5))
    shard = tables[0].shape[0] if not second else tables[8].shape[0]
    width = 4 * shard
    wanted = jnp.where(zl // 2 == zh, zl, (zl + 2) % 4)
    if second:
        wanted = wanted + 1 - 2 * (wanted % 2)

    def row_copy(src, slot, array):
        lanes = pl.ds(pl.multiple_of(slot * width, 128), width)
        return pltpu.make_async_copy(src, left.at[0, array, :, lanes], row_sem.at[slot, array])

    def table_copy(src, base, slot, q):
        at = pl.multiple_of(slot * width + q * shard, 32)
        return pltpu.make_async_copy(src.at[pl.ds(base, shard), :], tab.at[0, pl.ds(at, shard), :], tab_sem.at[slot, q])

    for n, dy in enumerate(STEPS_Y):
        chunk = (y + 4 + dy) % 4

        @pl.when(chunk // 2 == wanted % 2)
        def _(n=n, chunk=chunk):
            for array in range(2):
                row_copy(rows[2 * n + array], chunk % 2, array).start()
    for k, group, base in (((1, 0, 0), (3, 1, 0)) if second else ((0, 0, 0), (2, 1, 1))):
        @pl.when((zl + 4 - k) % 4 == wanted)
        def _(group=group, base=base):
            for j, dx in enumerate(STEPS_X):
                xs = (x + 4 + dx) % 4
                for other in range(2):
                    src = tables[8 * group + 2 * j + other]
                    table_copy(src, base * shard, xs // 2, (xs % 2) * 2 + (c + other) % 2).start()
    acc[...] = before[0][...] if before else jnp.zeros_like(acc)
    for slot in range(2):
        for array in range(2):
            row_copy(rows[0], slot, array).wait()
        for q in range(4):
            table_copy(tables[0], 0, slot, q).wait()
    pair_products(0, left, tab, acc)


def sum_kernel(half, span, places, n_tables, n_sums, where_ref, *refs):
    rows, tables = refs[:len(places)], refs[len(places):len(places) + n_tables]
    before, (sum_ref, *scratch) = refs[len(places) + n_tables:][:n_sums], refs[len(places) + n_tables + n_sums:]
    sum_ref[...] = before[0][...]
    multiply(half, span, places, where_ref, rows, tables, sum_ref, *scratch)


def last_kernel(half, span, places, n_tables, where_ref, *refs):
    rows, tables = refs[:len(places)], refs[len(places):len(places) + n_tables]
    before_ref, dec_ref, top_ref, acc, *scratch = refs[len(places) + n_tables:]
    acc[...] = before_ref[...]
    multiply(half, span, places, where_ref, rows, tables, acc, *scratch)
    tall = 32

    def fit(b, carry):
        at = pl.ds(pl.multiple_of(b * tall, tall), tall)
        dec_ref[at, :] = fit_gain(lambda p: acc[at, 512 + p * 128:512 + (p + 1) * 128],
                                  lambda k: acc[at, k * 128:(k + 1) * 128])
        return carry

    lax.fori_loop(0, acc.shape[0] // tall, fit, 0)
    top = jnp.max(dec_ref[...].T, axis=0, keepdims=True)
    top_ref[...] = jnp.broadcast_to(top, top_ref.shape)


def run(kernel, where, rows, tables, sums, outs, pairs, height, width, keep=()):
    vmem = pl.BlockSpec(memory_space=pltpu.VMEM)
    return pl.pallas_call(
        kernel,
        out_shape=outs,
        in_specs=[pl.BlockSpec(memory_space=pltpu.SMEM)]
        + [pl.BlockSpec(memory_space=pl.ANY)] * (len(rows) + len(tables)) + [vmem] * len(sums),
        out_specs=(vmem,) * len(outs),
        input_output_aliases={1 + len(rows) + len(tables): 0} if sums and len(outs) == 1 else {},
        scratch_shapes=list(keep) + [
            pltpu.VMEM((pairs, 2, height, 2 * width), jnp.bfloat16),
            pltpu.VMEM((pairs, 2 * width, 512), jnp.bfloat16),
            pltpu.SemaphoreType.DMA((2, 2) if pairs == 1 else (len(rows),)),
            pltpu.SemaphoreType.DMA((2 * pairs, 4)),
        ],
        compiler_params=pltpu.CompilerParams(vmem_limit_bytes=24 << 20),
        cost_estimate=pl.CostEstimate(
            flops=2 * height * 2 * pairs * width * 1792, bytes_accessed=pairs << 22, transcendentals=0),
    )(where, *rows, *tables, *sums)


def spread_x(block):
    return [block] + [shift(block, dx=dx) for dx in (1, -1, 2)]


def spread_and_fit(flux, ivar, mask, table):
    gz, spec = lax.axis_index("gz"), lax.axis_index("spec")
    where = jnp.stack([gz // 4, gz % 4, spec // 8, spec // 2 % 4, spec % 2]).astype(jnp.int32)
    shard = table.shape[0]
    flat = table.reshape(shard, 4 * table.shape[2])
    ivar_f = ivar.astype(jnp.float32)
    mask_f = mask.astype(jnp.float32)
    wt = (ivar_f * mask_f).astype(jnp.bfloat16)
    wd = (flux.astype(jnp.float32) * ivar_f * mask_f).astype(jnp.bfloat16)

    two = jnp.concatenate([shift(flat, dl=1), shift(flat, dl=2)], axis=0)
    last = shift(flat, dl=3)
    tables = []
    for block in (flat, two, last):
        for piece in spread_x(block):
            tables += [piece, shift(piece, dc=1)]

    yu, yd = [[shift(w, dy=dy) for w in (wd, wt)] for dy in (1, -1)]
    fu, fd = shift(yu[0], dy=1), shift(yd[1], dy=-1)
    za = shift(jnp.stack([wd[:, :CUT], wt[:, :CUT]]), dh=1)
    zb = shift(jnp.stack([wd[:, CUT:], wt[:, CUT:]]), dh=1)
    ua, da = shift(za, dy=1), shift(za, dy=-1)
    ya = [shift(ua[0], dy=1), shift(da[1], dy=-1)]
    ub, db, yb = shift(zb, dy=1), shift(zb, dy=-1), shift(zb, dy=2)

    spectra, width = wt.shape
    sums = jax.ShapeDtypeStruct((spectra, 14 * 128), jnp.float32)
    near, mid, far = tables[:8], tables[8:16], tables[16:]
    rows = [wd, wt, *yu, *yd, fu, fd]
    total, = run(functools.partial(block_kernel, False, 8, 16, 0), where, rows, near + mid, [],
                 (sums,), 1, spectra, width)
    total, = run(functools.partial(block_kernel, True, 8, 16, 1), where, rows, mid + far, [total],
                 (sums,), 1, spectra, width)
    places = [(n, None) for n in range(4)]
    total, = run(functools.partial(sum_kernel, 1, (0, CUT), places[:3] + [(3, 0), (3, 1)], 24, 1), where, [za, ua, da, *ya],
                 tables, [total], (sums,), 2, spectra, CUT)
    decrease, top = run(
        functools.partial(last_kernel, 1, (CUT, width - CUT), places, 24), where, [zb, ub, db, yb], tables, [total],
        (jax.ShapeDtypeStruct((spectra, 128), jnp.float32), jax.ShapeDtypeStruct((8, spectra), jnp.float32)),
        2, spectra, width - CUT, keep=[pltpu.VMEM(sums.shape, sums.dtype)])
    tops = lax.all_to_all(top, "gz", 0, 0, tiled=True)
    return decrease, jnp.max(tops, axis=0)


def solution(mesh):
    placed = (P("spec", "gz"), P("spec", "gz"), P("spec", "gz"), P("spec", None, "gz"))
    return jax.shard_map(
        spread_and_fit, mesh=mesh, in_specs=placed, out_specs=(P("spec", "gz"), P("spec")), check_vma=False
    )
```

```python
import functools

import jax
import jax.numpy as jnp
from jax import lax
from jax.experimental import pallas as pl
from jax.experimental.pallas import tpu as pltpu
from jax.sharding import PartitionSpec as P


PAIR_LIST = ((0, 0), (0, 1), (0, 2), (0, 3), (1, 1), (1, 2), (1, 3), (2, 2), (2, 3), (3, 3))
AXES = ("gz", "spec")
NZH, NY, NZL, NX = 2, 4, 4, 4
STEPS_Y = (0, -1, 1, 2)
STEPS_X = (0, -1, 1, 2)
CUT = 640


def place(i):
    gz, spec = divmod(i, NZL * NX * 2)
    zh, y = divmod(gz, NY)
    zl, r = divmod(spec, NX * 2)
    x, c = divmod(r, 2)
    return zh, y, zl, x, c


def number(zh, y, zl, x, c):
    return ((zh % NZH) * NY + y % NY) * NZL * NX * 2 + (zl % NZL) * NX * 2 + (x % NX) * 2 + c % 2


def shift(value, dh=0, dy=0, dl=0, dx=0, dc=0):
    pairs = []
    for i in range(NZH * NY * NZL * NX * 2):
        zh, y, zl, x, c = place(i)
        pairs.append((i, number(zh + dh, y + dy, zl + dl, x + dx, c + dc)))
    return lax.ppermute(value, AXES, pairs)


def fit_gain(gram, proj):
    where = {}
    for n, pair in enumerate(PAIR_LIST):
        where[pair] = n
    lower = {}
    for j in range(4):
        diag = gram(where[j, j])
        for k in range(j):
            diag = diag - lower[j, k] * lower[j, k]
        lower[j, j] = jnp.sqrt(diag)
        for i in range(j + 1, 4):
            entry = gram(where[j, i])
            for k in range(j):
                entry = entry - lower[i, k] * lower[j, k]
            lower[i, j] = entry / lower[j, j]
    solved = []
    total = None
    for i in range(4):
        value = proj(i)
        for k in range(i):
            value = value - lower[i, k] * solved[k]
        value = value / lower[i, i]
        solved.append(value)
        total = value * value if total is None else total + value * value
    return total


def pair_products(m, left, tab, acc):
    lhs = left[m, 0]
    for t in range(2):
        at = slice(t * 256, (t + 1) * 256)
        acc[:, at] += jnp.dot(lhs, tab[m, :, at], preferred_element_type=jnp.float32)
    lhs = left[m, 1]

    def comp(i):
        return tab[m, :, i * 128:(i + 1) * 128]

    for t in range(5):
        (a, b), (e, f) = PAIR_LIST[2 * t], PAIR_LIST[2 * t + 1]
        right = jnp.concatenate([comp(a) * comp(b), comp(e) * comp(f)], axis=1)
        at = slice(512 + t * 256, 512 + (t + 1) * 256)
        acc[:, at] += jnp.dot(lhs, right, preferred_element_type=jnp.float32)


def multiply(half, span, places, where_ref, rows, tables, acc, left, tab, row_sem, tab_sem):
    zh, y, zl, x, c = (where_ref[i] for i in range(5))
    shard = tables[0].shape[0]
    first, width = span
    near, mid, far = tables[:8], tables[8:16], tables[16:]
    pieces = []
    for q in range(4):
        low, high = max(first, q * shard), min(first + width, (q + 1) * shard)
        pieces.append((low - q * shard, high - low, low - first) if low < high else None)

    def table_copy(src, base, n, q):
        start, size, to = pieces[q]
        at = pl.multiple_of((n % 2) * width + to, 32)
        return pltpu.make_async_copy(
            src.at[pl.ds(base + start, size), :], tab.at[n // 2, pl.ds(at, size), :], tab_sem.at[n, q])

    def row_copy(src, m, i, array):
        return pltpu.make_async_copy(
            src, left.at[m, array, :, pl.ds(i * width, width)], row_sem.at[2 * m + i, array])

    for m, (n, array) in enumerate(places):
        for part in (0, 1) if array is None else (array,):
            row_copy(rows[m].at[part] if array is None else rows[m], n // 2, n % 2, part).start()
    for k in range(4):
        zs = (zl + 4 - k) % 4

        @pl.when(zs // 2 == (zh + half) % 2)
        def _(k=k, zs=zs):
            for j, dx in enumerate(STEPS_X):
                xs = (x + 4 + dx) % 4
                dy = ((zs % 2) * 2 + xs // 2 + 4 - y) % 4
                n = jnp.where(dy == 0, 0, jnp.where(dy == 3, 1, jnp.where(dy == 1, 2, 3)))
                for other in range(2):
                    src = (near, mid, mid, far)[k][2 * j + other]
                    base = shard if k == 2 else 0
                    mine = (xs % 2) * 2 + (c + other) % 2
                    if width == 4 * shard:
                        at = pl.multiple_of((n % 2) * width + mine * shard, 32)
                        pltpu.make_async_copy(
                            src.at[pl.ds(base, shard), :], tab.at[n // 2, pl.ds(at, shard), :], tab_sem.at[n, mine]).start()
                        continue
                    for q in range(4):
                        if pieces[q] is not None:
                            @pl.when(mine == q)
                            def _(src=src, base=base, n=n, q=q):
                                table_copy(src, base, n, q).start()
    sample = rows[0].at[0] if places[0][1] is None else rows[0]

    def step(m, carry):
        for i in range(2):
            for array in range(2):
                row_copy(sample, m, i, array).wait()
            for q in range(4):
                if pieces[q] is not None:
                    start, size, to = pieces[q]
                    pltpu.make_async_copy(
                        far[0].at[pl.ds(start, size), :], tab.at[m, pl.ds(i * width + to, size), :],
                        tab_sem.at[2 * m + i, q]).wait()
        pair_products(m, left, tab, acc)
        return carry

    lax.fori_loop(0, 2, step, 0)


def block_kernel(second, n_rows, n_tables, n_sums, where_ref, *refs):
    rows, tables = refs[:n_rows], refs[n_rows:n_rows + n_tables]
    before = refs[n_rows + n_tables:n_rows + n_tables + n_sums]
    acc, left, tab, row_sem, tab_sem = refs[n_rows + n_tables + n_sums:]
    zh, y, zl, x, c = (where_ref[i] for i in range(5))
    shard = tables[0].shape[0] if not second else tables[8].shape[0]
    width = 4 * shard
    wanted = jnp.where(zl // 2 == zh, zl, (zl + 2) % 4)
    if second:
        wanted = wanted + 1 - 2 * (wanted % 2)

    def row_copy(src, slot, array):
        lanes = pl.ds(pl.multiple_of(slot * width, 128), width)
        return pltpu.make_async_copy(src, left.at[0, array, :, lanes], row_sem.at[slot, array])

    def table_copy(src, base, slot, q):
        at = pl.multiple_of(slot * width + q * shard, 32)
        return pltpu.make_async_copy(src.at[pl.ds(base, shard), :], tab.at[0, pl.ds(at, shard), :], tab_sem.at[slot, q])

    for n, dy in enumerate(STEPS_Y):
        chunk = (y + 4 + dy) % 4

        @pl.when(chunk // 2 == wanted % 2)
        def _(n=n, chunk=chunk):
            for array in range(2):
                row_copy(rows[2 * n + array], chunk % 2, array).start()
    for k, group, base in (((1, 0, 0), (3, 1, 0)) if second else ((0, 0, 0), (2, 1, 1))):
        @pl.when((zl + 4 - k) % 4 == wanted)
        def _(group=group, base=base):
            for j, dx in enumerate(STEPS_X):
                xs = (x + 4 + dx) % 4
                for other in range(2):
                    src = tables[8 * group + 2 * j + other]
                    table_copy(src, base * shard, xs // 2, (xs % 2) * 2 + (c + other) % 2).start()
    acc[...] = before[0][...] if before else jnp.zeros_like(acc)
    for slot in range(2):
        for array in range(2):
            row_copy(rows[0], slot, array).wait()
        for q in range(4):
            table_copy(tables[0], 0, slot, q).wait()
    pair_products(0, left, tab, acc)


def sum_kernel(half, span, places, n_tables, n_sums, where_ref, *refs):
    rows, tables = refs[:len(places)], refs[len(places):len(places) + n_tables]
    before, (sum_ref, *scratch) = refs[len(places) + n_tables:][:n_sums], refs[len(places) + n_tables + n_sums:]
    sum_ref[...] = before[0][...]
    multiply(half, span, places, where_ref, rows, tables, sum_ref, *scratch)


def last_kernel(half, span, places, n_tables, where_ref, *refs):
    rows, tables = refs[:len(places)], refs[len(places):len(places) + n_tables]
    before_ref, dec_ref, top_ref, acc, *scratch = refs[len(places) + n_tables:]
    acc[...] = before_ref[...]
    multiply(half, span, places, where_ref, rows, tables, acc, *scratch)
    tall = 32

    def fit(b, carry):
        at = pl.ds(pl.multiple_of(b * tall, tall), tall)
        dec_ref[at, :] = fit_gain(lambda p: acc[at, 512 + p * 128:512 + (p + 1) * 128],
                                  lambda k: acc[at, k * 128:(k + 1) * 128])
        return carry

    lax.fori_loop(0, acc.shape[0] // tall, fit, 0)
    top = jnp.max(dec_ref[...].T, axis=0, keepdims=True)
    top_ref[...] = jnp.broadcast_to(top, top_ref.shape)


def run(kernel, where, rows, tables, sums, outs, pairs, height, width, keep=()):
    vmem = pl.BlockSpec(memory_space=pltpu.VMEM)
    return pl.pallas_call(
        kernel,
        out_shape=outs,
        in_specs=[pl.BlockSpec(memory_space=pltpu.SMEM)]
        + [pl.BlockSpec(memory_space=pl.ANY)] * (len(rows) + len(tables)) + [vmem] * len(sums),
        out_specs=(vmem,) * len(outs),
        input_output_aliases={1 + len(rows) + len(tables): 0} if sums and len(outs) == 1 else {},
        scratch_shapes=list(keep) + [
            pltpu.VMEM((pairs, 2, height, 2 * width), jnp.bfloat16),
            pltpu.VMEM((pairs, 2 * width, 512), jnp.bfloat16),
            pltpu.SemaphoreType.DMA((2 * pairs, 2)),
            pltpu.SemaphoreType.DMA((2 * pairs, 4)),
        ],
        compiler_params=pltpu.CompilerParams(vmem_limit_bytes=24 << 20),
        cost_estimate=pl.CostEstimate(
            flops=2 * height * 2 * pairs * width * 1792, bytes_accessed=pairs << 22, transcendentals=0),
    )(where, *rows, *tables, *sums)


def spread_x(block):
    return [block] + [shift(block, dx=dx) for dx in (1, -1, 2)]


def spread_and_fit(flux, ivar, mask, table):
    gz, spec = lax.axis_index("gz"), lax.axis_index("spec")
    where = jnp.stack([gz // 4, gz % 4, spec // 8, spec // 2 % 4, spec % 2]).astype(jnp.int32)
    shard = table.shape[0]
    flat = table.reshape(shard, 4 * table.shape[2])
    ivar_f = ivar.astype(jnp.float32)
    mask_f = mask.astype(jnp.float32)
    wt = (ivar_f * mask_f).astype(jnp.bfloat16)
    wd = (flux.astype(jnp.float32) * ivar_f * mask_f).astype(jnp.bfloat16)

    two = jnp.concatenate([shift(flat, dl=1), shift(flat, dl=2)], axis=0)
    last = shift(flat, dl=3)
    tables = []
    for block in (flat, two, last):
        for piece in spread_x(block):
            tables += [piece, shift(piece, dc=1)]

    yu, yd = [[shift(w, dy=dy) for w in (wd, wt)] for dy in (1, -1)]
    fu, fd = shift(yu[0], dy=1), shift(yd[1], dy=-1)
    za = shift(jnp.stack([wd[:, :CUT], wt[:, :CUT]]), dh=1)
    zb = shift(jnp.stack([wd[:, CUT:], wt[:, CUT:]]), dh=1)
    ua, da = shift(za, dy=1), shift(za, dy=-1)
    ya = [shift(ua[0], dy=1), shift(da[1], dy=-1)]
    ub, db, yb = shift(zb, dy=1), shift(zb, dy=-1), shift(zb, dy=2)

    spectra, width = wt.shape
    sums = jax.ShapeDtypeStruct((spectra, 14 * 128), jnp.float32)
    near, mid, far = tables[:8], tables[8:16], tables[16:]
    rows = [wd, wt, *yu, *yd, fu, fd]
    total, = run(functools.partial(block_kernel, False, 8, 16, 0), where, rows, near + mid, [],
                 (sums,), 1, spectra, width)
    total, = run(functools.partial(block_kernel, True, 8, 16, 1), where, rows, mid + far, [total],
                 (sums,), 1, spectra, width)
    places = [(n, None) for n in range(4)]
    total, = run(functools.partial(sum_kernel, 1, (0, CUT), places[:3] + [(3, 0), (3, 1)], 24, 1), where, [za, ua, da, *ya],
                 tables, [total], (sums,), 2, spectra, CUT)
    decrease, top = run(
        functools.partial(last_kernel, 1, (CUT, width - CUT), places, 24), where, [zb, ub, db, yb], tables, [total],
        (jax.ShapeDtypeStruct((spectra, 128), jnp.float32), jax.ShapeDtypeStruct((8, spectra), jnp.float32)),
        2, spectra, width - CUT, keep=[pltpu.VMEM(sums.shape, sums.dtype)])
    tops = lax.all_to_all(top, "gz", 0, 0, tiled=True)
    return decrease, jnp.max(tops, axis=0)


def solution(mesh):
    placed = (P("spec", "gz"), P("spec", "gz"), P("spec", "gz"), P("spec", None, "gz"))
    return jax.shard_map(
        spread_and_fit, mesh=mesh, in_specs=placed, out_specs=(P("spec", "gz"), P("spec")), check_vma=False
    )
```
